32 devices in a mesh: groups: 1, kcol: 16 (over z, y, x), qrow: 2 (over core).
Axes of the slice: x: 2, y: 2, z: 4, core: 2. Of those that a mesh axis runs over, the one named last changes fastest.
Arguments:
- queries: bfloat16 [128, 1024], P(('groups', 'kcol', 'qrow')), may hold values from -120 to 120
- key_value: bfloat16 [24576, 256], P(('groups', 'kcol')), may hold values from -6 to 6
- block_lists: int32 [1, 64], P('groups'), may hold values from 0 to 191, as said below
Outputs:
- attended: bfloat16 [128, 1024], P(('groups', 'kcol', 'qrow'))
The draws below stay inside these ranges and needn't reach their ends.
Inputs may be any that keep to these rules, and one draw needn't show every extreme that they name: `block_lists`: row i names 64 distinct key blocks, none after block 191 + i (the block that holds query block i); it always names that block, the 11 blocks just before it, and block 0.
All inputs are finite; a program needn't handle non-finite values.
Results may differ from the reference program's by a relative error of at most 0.0065.
Values may be sent and summed in bfloat16 or wider, within the bound.
No kernel may reach another device: no remote copies, remote signals or barrier semaphores. Data moves between devices by JAX's collectives and lax.ppermute only.
A program may use at most 128 MiB of HBM per device.

```python
import math
import jax
import jax.numpy as jnp
from jax import lax

HD = 128
HEADS = 8
BLK = 128
KB_DEV = 12
KB = 192
QTOK = 128
QB = 1
NSEL = 64


def draw_pairs(key):
    key_rows = jnp.clip(jax.random.normal(jax.random.fold_in(key, 11), (KB * BLK, HD), jnp.float32), -6.0, 6.0)
    value_rows = jnp.clip(jax.random.normal(jax.random.fold_in(key, 12), (KB * BLK, HD), jnp.float32), -6.0, 6.0)
    return (key_rows, value_rows)


def draw_key_value(key, part):
    key_rows, value_rows = draw_pairs(key)
    return jnp.concatenate([key_rows, value_rows], axis=1).astype(jnp.bfloat16)


def draw_queries(key, part):
    drawn = 3.0 * jnp.clip(jax.random.normal(jax.random.fold_in(key, 14), (QTOK, HEADS, HD), jnp.float32), -6.0, 6.0)
    return drawn.reshape(QTOK, HEADS * HD).astype(jnp.bfloat16)


def draw_block_lists(key, part):
    popular = (jax.random.randint(jax.random.fold_in(key, 21), (KB,), 0, 4) == 0).astype(jnp.int32)
    row_noise = jax.random.randint(jax.random.fold_in(key, 22), (QB, KB), 0, 65536)
    candidates = jnp.arange(KB, dtype=jnp.int32)

    def one_row(block_index, noise_row):
        limit = KB - QB + block_index - KB_DEV + 1
        score = (popular * 65536 + noise_row) * 4096 + candidates
        score = jnp.where(candidates == 0, 2 ** 30, score)
        score = jnp.where(candidates < limit, score, -1 - candidates)
        unused, picked = lax.top_k(score, NSEL - KB_DEV)
        window = limit + jnp.arange(KB_DEV, dtype=jnp.int32)
        return jnp.concatenate([picked.astype(jnp.int32), window])
    return jax.vmap(one_row)(jnp.arange(QB, dtype=jnp.int32), row_noise)


def setup_inputs(seed: int = 0, part: int = 0) -> dict:
    splits = jax.random.split(jax.random.key(seed), 4)
    own_keys = jax.random.split(jax.random.fold_in(splits[3], part), 4)
    return {
        "queries": draw_queries(jax.random.fold_in(jax.random.fold_in(splits[3], part), 71), part),
        "key_value": draw_key_value(jax.random.fold_in(jax.random.fold_in(splits[3], part), 71), part),
        "block_lists": draw_block_lists(jax.random.fold_in(jax.random.fold_in(splits[3], part), 71), part),
    }


masked_score = -1e+30

def reference(queries, key_value, block_lists):
    score_scale = 1.0 / math.sqrt(HD)
    blocks = key_value.reshape(KB, BLK, 2 * HD)
    offset = (KB - QB) * BLK
    query_tiles = queries.reshape(QB, BLK, HEADS, HD)

    def one_block(inputs):
        query_tile, listed, block_index = inputs
        chosen = jnp.take(blocks, listed, axis=0).reshape(NSEL * BLK, 2 * HD).astype(jnp.float32)
        key_pos = (listed[:, None] * BLK + jnp.arange(BLK, dtype=jnp.int32)[None, :]).reshape(-1)
        query_pos = offset + block_index * BLK + jnp.arange(BLK, dtype=jnp.int32)
        visible = key_pos[None, :] <= query_pos[:, None]
        scores = jnp.einsum('thd,kd->htk', query_tile.astype(jnp.float32), chosen[:, :HD], precision=lax.Precision.HIGHEST) * score_scale
        scores = jnp.where(visible[None], scores, masked_score)
        row_max = lax.optimization_barrier(jnp.max(scores, axis=-1))
        weights = jnp.where(visible[None], jnp.exp(scores - row_max[..., None]), 0.0)
        row_total = lax.optimization_barrier(jnp.sum(weights, axis=-1))
        rounded = lax.optimization_barrier(weights.astype(jnp.bfloat16)).astype(jnp.float32)
        numerator = jnp.einsum('htk,kd->thd', rounded, chosen[:, HD:], precision=lax.Precision.HIGHEST)
        result = numerator / jnp.transpose(row_total)[..., None]
        return result.reshape(BLK, HEADS * HD).astype(jnp.bfloat16)
    attended = lax.map(one_block, (query_tiles, block_lists, jnp.arange(QB, dtype=jnp.int32)))
    return attended.reshape(QTOK, HEADS * HD)
```

```python
import functools
import math

import jax
import jax.numpy as jnp
from jax import lax
from jax.experimental import pallas as pl
from jax.experimental.pallas import tpu as pltpu
from jax.sharding import PartitionSpec as P


BLK = 128
LANES = 128
hidden_score = -1e30
floor_score = -1e29


def swap_pairs(size, mask):
    return [(i, i ^ mask) for i in range(size)]


def attend_kernel(plan, info, *refs):
    tokens, heads, dim, groups, masks, tok_dev, row_count, first_query, spans = plan
    q_parts, kv_parts, (keep, send, scores) = refs[:2], refs[2:-3], refs[-3:]
    rows = heads * tokens
    scale = math.log2(math.e) / math.sqrt(dim)
    blocks = [(part, i) for part, ref in enumerate(kv_parts) for i in range(ref.shape[0] // BLK)]
    count = len(blocks)
    query = jnp.concatenate(
        [
            jnp.concatenate([part[:, h * dim : (h + 1) * dim] for part in q_parts], axis=0)
            for h in range(heads)
        ],
        axis=0,
    )
    column, row_index = info[(groups + 1) * count], info[(groups + 1) * count + 1]
    t = lax.rem(lax.broadcasted_iota(jnp.int32, (rows, BLK), 0), tokens)
    source = lax.div(t, tok_dev)
    relative = jnp.zeros_like(t)
    for k, mask in enumerate(masks):
        relative += ((source >> k) & 1) * mask
    token = ((relative ^ column) * row_count + row_index) * tok_dev + lax.rem(t, tok_dev)
    lane = lax.broadcasted_iota(jnp.int32, (rows, BLK), 1)

    def bias_of(b):
        out = jnp.where(info[b] > 0, 0.0, hidden_score).astype(jnp.float32)
        for g in range(1, groups):
            other = jnp.where(info[g * count + b] > 0, 0.0, hidden_score).astype(jnp.float32)
            out = jnp.where(lax.div(token, BLK) == g, other, out)
        return out

    top = jnp.full((rows, BLK), floor_score, jnp.float32)
    for b, (part, i) in enumerate(blocks):
        keys = kv_parts[part][i * BLK : (i + 1) * BLK, :dim]
        s = lax.dot_general(
            query, keys, (((1,), (1,)), ((), ())), preferred_element_type=jnp.float32
        )
        s = s + bias_of(b)
        if i >= spans[part]:
            key_pos = info[groups * count + b] * BLK + lane
            s = jnp.where(key_pos <= first_query + token, s, hidden_score)
        scores[:, b * BLK : (b + 1) * BLK] = s
        top = jnp.maximum(top, s)
    row_max = jnp.max(top, axis=1, keepdims=True)
    total = jnp.zeros((rows, BLK), jnp.float32)
    numer = jnp.zeros((rows, dim), jnp.float32)
    base = 0
    for ref in kv_parts:
        width = ref.shape[0]
        weights = jnp.exp2((scores[:, base : base + width] - row_max) * scale)
        for i in range(width // BLK):
            total += weights[:, i * BLK : (i + 1) * BLK]
        numer += jnp.dot(
            weights.astype(jnp.bfloat16), ref[:, dim:], preferred_element_type=jnp.float32
        )
        base += width
    row_total = jnp.sum(total, axis=1, keepdims=True)
    stat_lane = lax.broadcasted_iota(jnp.int32, (tokens, LANES), 1)
    stats = jnp.zeros((tokens, LANES), jnp.float32)
    half = tokens // 2
    for h in range(heads):
        at = slice(h * tokens, (h + 1) * tokens)
        stats = jnp.where(stat_lane == h, row_max[at], stats)
        stats = jnp.where(stat_lane == heads + h, row_total[at], stats)
        part = numer[at]
        keep[:, h * dim : (h + 1) * dim] = part[:half]
        send[:, h * dim : (h + 1) * dim] = part[half:]
    keep[:, heads * dim :] = stats[:half]
    send[:, heads * dim :] = stats[half:]


def combine(heads, dim, left, right):
    scale = math.log2(math.e) / math.sqrt(dim)
    feature = heads * dim
    stat_left, stat_right = left[:, feature:], right[:, feature:]
    top = jnp.maximum(stat_left, stat_right)
    lane = lax.broadcasted_iota(jnp.int32, top.shape, 1)
    is_max = lane < heads
    shrink_left = jnp.where(is_max, jnp.exp2((stat_left - top) * scale), 0.0)
    shrink_right = jnp.where(is_max, jnp.exp2((stat_right - top) * scale), 0.0)
    moved_left = pltpu.roll(shrink_left, heads, 1)
    moved_right = pltpu.roll(shrink_right, heads, 1)
    stats = jnp.where(is_max, top, stat_left * moved_left + stat_right * moved_right)
    parts = [
        left[:, h * dim : (h + 1) * dim] * shrink_left[:, h : h + 1]
        + right[:, h * dim : (h + 1) * dim] * shrink_right[:, h : h + 1]
        for h in range(heads)
    ]
    return parts, stats


def merge_kernel(heads, dim, left, right, keep, send):
    parts, stats = combine(heads, dim, left, right)
    half = keep.shape[0]
    for h, part in enumerate(parts):
        keep[:, h * dim : (h + 1) * dim] = part[:half]
        send[:, h * dim : (h + 1) * dim] = part[half:]
    keep[:, heads * dim :] = stats[:half]
    send[:, heads * dim :] = stats[half:]


def finish_kernel(heads, dim, left, right, out):
    parts, stats = combine(heads, dim, left, right)
    for h, part in enumerate(parts):
        total = stats[:, heads + h : heads + h + 1]
        out[:, h * dim : (h + 1) * dim] = (part / total).astype(out.dtype)


def in_vmem():
    return pl.BlockSpec(memory_space=pltpu.VMEM)


def per_device(queries, key_value, block_lists):
    columns = lax.axis_size("kcol")
    column = lax.axis_index("kcol")
    row_count = lax.axis_size("qrow")
    row_index = lax.axis_index("qrow")
    tok_dev, feature = queries.shape
    dim = key_value.shape[1] // 2
    heads = feature // dim
    stored = key_value.shape[0] // BLK
    groups = block_lists.shape[0]
    first_query = (stored * columns - groups) * BLK
    masks = [columns >> k for k in range(1, columns.bit_length() - 1)]
    half = stored // 2

    gathered = queries
    for mask in masks:
        arrived = lax.ppermute(gathered, "kcol", swap_pairs(columns, mask))
        if mask != masks[-1]:
            gathered = jnp.concatenate([gathered, arrived], axis=0)
    tokens = 2 * gathered.shape[0]

    mine = lax.dynamic_slice_in_dim(key_value, row_index * half * BLK, half * BLK, 0)
    near = lax.ppermute(mine, "kcol", swap_pairs(columns, 1))
    far = lax.ppermute(near, "qrow", swap_pairs(row_count, 1))

    local = jnp.arange(stored, dtype=jnp.int32)
    other = (column ^ 1) * stored
    ids = jnp.concatenate(
        [
            column * stored + local,
            other + row_index * half + local[:half],
            other + (1 - row_index) * half + local[:half],
        ]
    )
    listed = jnp.any(block_lists[:, :, None] == ids[None, None, :], axis=1).astype(jnp.int32)
    info = jnp.concatenate([listed.reshape(-1), ids, jnp.stack([column, row_index]).astype(jnp.int32)])

    spans = (max(stored - groups, 0), max(half - groups, 0), max(half - groups, 0))
    plan = (tokens, heads, dim, groups, tuple(masks), tok_dev, row_count, first_query, spans)
    width = feature + LANES
    rows = tokens // 2
    message = jax.ShapeDtypeStruct((rows, width), jnp.float32)
    keep, send = pl.pallas_call(
        functools.partial(attend_kernel, plan),
        out_shape=(message, message),
        in_specs=[pl.BlockSpec(memory_space=pltpu.SMEM)] + [in_vmem()] * 5,
        out_specs=(in_vmem(), in_vmem()),
        scratch_shapes=[pltpu.VMEM((heads * tokens, 2 * stored * BLK), jnp.float32)],
        compiler_params=pltpu.CompilerParams(vmem_limit_bytes=32 * 2**20),
        name="attend",
    )(info, gathered, arrived, key_value, near, far)

    for mask in reversed(masks):
        arrived = lax.ppermute(send, "kcol", swap_pairs(columns, mask))
        if mask != masks[0]:
            rows //= 2
            message = jax.ShapeDtypeStruct((rows, width), jnp.float32)
            keep, send = pl.pallas_call(
                functools.partial(merge_kernel, heads, dim),
                out_shape=(message, message),
                in_specs=[in_vmem()] * 2,
                out_specs=(in_vmem(), in_vmem()),
                compiler_params=pltpu.CompilerParams(vmem_limit_bytes=8 * 2**20),
                name="merge",
            )(keep, arrived)
    return pl.pallas_call(
        functools.partial(finish_kernel, heads, dim),
        out_shape=jax.ShapeDtypeStruct((tok_dev, feature), jnp.bfloat16),
        in_specs=[in_vmem()] * 2,
        out_specs=in_vmem(),
        compiler_params=pltpu.CompilerParams(vmem_limit_bytes=8 * 2**20),
        name="finish",
    )(keep, arrived)


def solution(mesh):
    placed = (P(("groups", "kcol", "qrow"), None), P(("groups", "kcol"), None), P("groups", None))
    return jax.shard_map(
        per_device,
        mesh=mesh,
        in_specs=placed,
        out_specs=P(("groups", "kcol", "qrow"), None),
        check_vma=False,
    )
```

```python
import functools
import math

import jax
import jax.numpy as jnp
from jax import lax
from jax.experimental import pallas as pl
from jax.experimental.pallas import tpu as pltpu
from jax.sharding import PartitionSpec as P


BLK = 128
LANES = 128
AXES = ("kcol", "qrow")
hidden_score = -1e30
floor_score = -1e29


def scale_of(dim):
    return math.log2(math.e) / math.sqrt(dim)


def token_of(plan, info, rows):
    tokens, tok_dev, row_count, masks = plan.tokens, plan.tok_dev, plan.row_count, plan.masks
    column, row_index = info[plan.tail], info[plan.tail + 1]
    t = lax.rem(lax.broadcasted_iota(jnp.int32, (rows, BLK), 0), tokens)
    source = lax.div(t, tok_dev)
    relative = jnp.zeros_like(t)
    crossed = jnp.zeros_like(t)
    for k, mask in enumerate(masks):
        bit = (source >> k) & 1
        relative += bit * mask
        crossed ^= bit
    return ((relative ^ column) * row_count + (crossed ^ row_index)) * tok_dev + lax.rem(t, tok_dev)


def block_scores(plan, info, query, kv, first, scores):
    rows = query.shape[0]
    token = token_of(plan, info, rows)
    lane = lax.broadcasted_iota(jnp.int32, (rows, BLK), 1)
    top = jnp.full((rows, BLK), floor_score, jnp.float32)
    for i in range(plan.stored):
        b = first + i
        bias = jnp.where(info[b] > 0, 0.0, hidden_score).astype(jnp.float32)
        for g in range(1, plan.groups):
            other = jnp.where(info[g * plan.count + b] > 0, 0.0, hidden_score).astype(jnp.float32)
            bias = jnp.where(lax.div(token, BLK) == g, other, bias)
        s = lax.dot_general(
            query,
            kv[i * BLK : (i + 1) * BLK, : plan.dim],
            (((1,), (1,)), ((), ())),
            preferred_element_type=jnp.float32,
        )
        s = s + bias
        if i >= plan.stored - plan.groups:
            key_pos = info[plan.groups * plan.count + b] * BLK + lane
            s = jnp.where(key_pos <= plan.first_query + token, s, hidden_score)
        scores[:, i * BLK : (i + 1) * BLK] = s
        top = jnp.maximum(top, s)
    return jnp.max(top, axis=1, keepdims=True)


def weigh(plan, scores, row_max, values):
    weights = jnp.exp2((scores[...] - row_max) * scale_of(plan.dim))
    total = weights[:, :BLK]
    for i in range(1, plan.stored):
        total = total + weights[:, i * BLK : (i + 1) * BLK]
    numer = jnp.dot(weights.astype(jnp.bfloat16), values, preferred_element_type=jnp.float32)
    return total, numer


def first_kernel(plan, info, first_half, second_half, kv, query_out, numer_out, max_out, total_out, scores):
    dim = plan.dim
    parts = (first_half, second_half)
    query = jnp.concatenate(
        [part[:, h * dim : (h + 1) * dim] for h in range(plan.heads) for part in parts], axis=0
    )
    row_max = block_scores(plan, info, query, kv, 0, scores)
    total, numer = weigh(plan, scores, row_max, kv[:, dim:])
    query_out[...] = query
    numer_out[...] = numer
    max_out[...] = jnp.broadcast_to(row_max, max_out.shape)
    total_out[...] = total


def second_kernel(plan, info, query, numer_in, max_in, total_in, kv, keep, send, scores):
    dim, heads, tokens = plan.dim, plan.heads, plan.tokens
    kv_max = block_scores(plan, info, query[...], kv, plan.stored, scores)
    row_max = jnp.maximum(kv_max, max_in[...])
    shrink = jnp.exp2((max_in[...] - row_max) * scale_of(dim))
    total, numer = weigh(plan, scores, row_max[:, :1], kv[:, dim:])
    numer = numer + numer_in[...] * shrink
    row_total = jnp.sum(total + total_in[...] * shrink, axis=1, keepdims=True)
    stat_lane = lax.broadcasted_iota(jnp.int32, (tokens, LANES), 1)
    stats = jnp.zeros((tokens, LANES), jnp.float32)
    half = tokens // 2
    for h in range(heads):
        at = slice(h * tokens, (h + 1) * tokens)
        stats = jnp.where(stat_lane == h, row_max[at], stats)
        stats = jnp.where(stat_lane == heads + h, row_total[at], stats)
        keep[:, h * dim : (h + 1) * dim] = numer[at][:half]
        send[:, h * dim : (h + 1) * dim] = numer[at][half:]
    keep[:, heads * dim :] = stats[:half]
    send[:, heads * dim :] = stats[half:]


def combine(heads, dim, left, right):
    feature = heads * dim
    stat_left, stat_right = left[:, feature:], right[:, feature:]
    top = jnp.maximum(stat_left, stat_right)
    lane = lax.broadcasted_iota(jnp.int32, top.shape, 1)
    is_max = lane < heads
    shrink_left = jnp.where(is_max, jnp.exp2((stat_left - top) * scale_of(dim)), 0.0)
    shrink_right = jnp.where(is_max, jnp.exp2((stat_right - top) * scale_of(dim)), 0.0)
    moved_left = pltpu.roll(shrink_left, heads, 1)
    moved_right = pltpu.roll(shrink_right, heads, 1)
    stats = jnp.where(is_max, top, stat_left * moved_left + stat_right * moved_right)
    parts = [
        left[:, h * dim : (h + 1) * dim] * shrink_left[:, h : h + 1]
        + right[:, h * dim : (h + 1) * dim] * shrink_right[:, h : h + 1]
        for h in range(heads)
    ]
    return parts, stats


def merge_kernel(heads, dim, left, right, keep, send):
    parts, stats = combine(heads, dim, left, right)
    half = keep.shape[0]
    for h, part in enumerate(parts):
        keep[:, h * dim : (h + 1) * dim] = part[:half]
        send[:, h * dim : (h + 1) * dim] = part[half:]
    keep[:, heads * dim :] = stats[:half]
    send[:, heads * dim :] = stats[half:]


def finish_kernel(heads, dim, left, right, out):
    parts, stats = combine(heads, dim, left, right)
    for h, part in enumerate(parts):
        total = stats[:, heads + h : heads + h + 1]
        out[:, h * dim : (h + 1) * dim] = (part / total).astype(out.dtype)


class Plan:
    def __init__(self, **sizes):
        self.__dict__.update(sizes)


def in_vmem(count):
    return [pl.BlockSpec(memory_space=pltpu.VMEM)] * count


def call(kernel, arguments, outputs, scalars=0, scratch=(), megabytes=8):
    return pl.pallas_call(
        kernel,
        out_shape=outputs,
        in_specs=[pl.BlockSpec(memory_space=pltpu.SMEM)] * scalars
        + in_vmem(len(arguments) - scalars),
        out_specs=tuple(in_vmem(len(outputs))),
        scratch_shapes=scratch,
        compiler_params=pltpu.CompilerParams(vmem_limit_bytes=megabytes * 2**20),
    )(*arguments)


def per_device(queries, key_value, block_lists):
    columns = lax.axis_size("kcol")
    column = lax.axis_index("kcol")
    row_count = lax.axis_size("qrow")
    row_index = lax.axis_index("qrow")
    tok_dev, feature = queries.shape
    dim = key_value.shape[1] // 2
    heads = feature // dim
    stored = key_value.shape[0] // BLK
    groups = block_lists.shape[0]
    masks = [columns >> k for k in range(1, columns.bit_length() - 1)]
    assert columns == 1 << (columns.bit_length() - 1) and row_count == 2

    def across(value, mask):
        pairs = [
            (c * row_count + r, (c ^ mask) * row_count + (r ^ 1))
            for c in range(columns)
            for r in range(row_count)
        ]
        return lax.ppermute(value, AXES, pairs)

    pairs = []
    for c in range(columns):
        pairs += [(c * row_count, (c ^ 1) * row_count + 1), (c * row_count + 1, c * row_count)]
    near = lax.ppermute(key_value, AXES, pairs)
    far = lax.ppermute(near, "qrow", [(0, 1), (1, 0)])

    local = jnp.arange(stored, dtype=jnp.int32)
    ids = jnp.concatenate(
        [(column ^ row_index) * stored + local, (column ^ row_index ^ 1) * stored + local]
    )
    count = 2 * stored
    listed = jnp.any(block_lists[:, :, None] == ids[None, None, :], axis=1).astype(jnp.int32)
    place = jnp.stack([column, row_index]).astype(jnp.int32)
    info = jnp.concatenate([listed.reshape(-1), ids, place])

    staged = lax.optimization_barrier(jnp.pad(queries, ((0, tok_dev), (0, 0))))
    gathered = queries
    for k, mask in enumerate(masks):
        arrived = across(gathered, mask)
        if k == 0 and mask != masks[-1]:
            gathered = staged.at[tok_dev:].set(arrived)
        elif mask != masks[-1]:
            gathered = jnp.concatenate([gathered, arrived], axis=0)
    tokens = 2 * gathered.shape[0]

    plan = Plan(
        tokens=tokens,
        heads=heads,
        dim=dim,
        groups=groups,
        masks=tuple(masks),
        tok_dev=tok_dev,
        row_count=row_count,
        stored=stored,
        count=count,
        tail=(groups + 1) * count,
        first_query=(stored * columns - groups) * BLK,
    )
    rows = heads * tokens

    def f32(*shape):
        return jax.ShapeDtypeStruct(shape, jnp.float32)

    scratch = [pltpu.VMEM((rows, stored * BLK), jnp.float32)]
    begun = call(
        functools.partial(first_kernel, plan),
        (info, gathered, arrived, near),
        (jax.ShapeDtypeStruct((rows, dim), jnp.bfloat16), f32(rows, dim), f32(rows, LANES), f32(rows, LANES)),
        scalars=1,
        scratch=scratch,
        megabytes=24,
    )
    size = tokens // 2
    width = feature + LANES
    keep, send = call(
        functools.partial(second_kernel, plan),
        (info, *begun, far),
        (f32(size, width), f32(size, width)),
        scalars=1,
        scratch=scratch,
        megabytes=24,
    )
    for mask in reversed(masks):
        arrived = across(send, mask)
        if mask != masks[0]:
            size //= 2
            keep, send = call(
                functools.partial(merge_kernel, heads, dim),
                (keep, arrived),
                (f32(size, width), f32(size, width)),
            )
    (out,) = call(
        functools.partial(finish_kernel, heads, dim),
        (keep, arrived),
        (jax.ShapeDtypeStruct((tok_dev, feature), jnp.bfloat16),),
    )
    return out


def solution(mesh):
    placed = (P(("groups", "kcol", "qrow"), None), P(("groups", "kcol"), None), P("groups", None))
    return jax.shard_map(
        per_device,
        mesh=mesh,
        in_specs=placed,
        out_specs=P(("groups", "kcol", "qrow"), None),
        check_vma=False,
    )
```

```python
import functools
import math

import jax
import jax.numpy as jnp
from jax import lax
from jax.experimental import pallas as pl
from jax.experimental.pallas import tpu as pltpu
from jax.sharding import PartitionSpec as P


BLK = 128
LANES = 128
AXES = ("kcol", "qrow")
hidden_score = -(2.0**100)
floor_score = -(2.0**96)


def scale_of(dim):
    return math.log2(math.e) / math.sqrt(dim)


def token_of(plan, rows, offset):
    column, row_index = lax.axis_index("kcol"), lax.axis_index("qrow")
    t = lax.broadcasted_iota(jnp.int32, (plan.half, BLK), 0) + offset
    source = lax.div(t, plan.tok_dev)
    relative = jnp.zeros_like(t)
    crossed = jnp.zeros_like(t)
    for k, mask in enumerate(plan.masks):
        bit = (source >> k) & 1
        relative += bit * mask
        crossed ^= bit
    place = (relative ^ column) * plan.row_count + (crossed ^ row_index)
    token = place * plan.tok_dev + lax.rem(t, plan.tok_dev)
    return jnp.concatenate([token] * (rows // plan.half), axis=0)


def block_scores(plan, bias, query, kv, part, offset, scores):
    rows = query.shape[0]
    token = token_of(plan, rows, offset)
    lane = lax.broadcasted_iota(jnp.int32, (rows, BLK), 1)
    origin = (lax.axis_index("kcol") ^ lax.axis_index("qrow") ^ part) * plan.stored
    top = jnp.full((rows, BLK), floor_score, jnp.float32)
    pack = 2 if plan.stored % 2 == 0 else 1
    for p in range(plan.stored // pack):
        wide = lax.dot_general(
            query,
            kv[p * pack * BLK : (p + 1) * pack * BLK, : plan.dim],
            (((1,), (1,)), ((), ())),
            preferred_element_type=jnp.float32,
        )
        for k in range(pack):
            i = p * pack + k
            b = part * plan.stored + i
            s = wide[:, k * BLK : (k + 1) * BLK]
            offset_row = bias[0, b : b + 1, :]
            for g in range(1, plan.groups):
                offset_row = jnp.where(lax.div(token, BLK) == g, bias[g, b : b + 1, :], offset_row)
            s = s + offset_row
            if i >= plan.stored - plan.groups:
                key_pos = (origin + i) * BLK + lane
                s = jnp.where(key_pos <= plan.first_query + token, s, hidden_score)
            scores[:, b * BLK : (b + 1) * BLK] = s
            top = jnp.maximum(top, s)
    return top


def weigh(plan, scores, first, row_max, values):
    at = slice(first * BLK, (first + plan.stored) * BLK)
    weights = jnp.exp2((scores[:, at] - row_max) * scale_of(plan.dim))
    total = weights[:, :BLK]
    for i in range(1, plan.stored):
        total = total + weights[:, i * BLK : (i + 1) * BLK]
    numer = jnp.dot(weights.astype(jnp.bfloat16), values, preferred_element_type=jnp.float32)
    return total, numer


def stack_heads(plan, tile):
    dim = plan.dim
    return jnp.concatenate([tile[:, h * dim : (h + 1) * dim] for h in range(plan.heads)], axis=0)


def stack_stats(plan, row_max, row_total):
    lane = lax.broadcasted_iota(jnp.int32, (plan.half, LANES), 1)
    stats = jnp.zeros((plan.half, LANES), jnp.float32)
    for h in range(plan.heads):
        at = slice(h * plan.half, (h + 1) * plan.half)
        stats = jnp.where(lane == h, row_max[at], stats)
        stats = jnp.where(lane == plan.heads + h, row_total[at], stats)
    return stats


def put_kept(out, parts, stats):
    dim = parts[0].shape[1]
    for h, part in enumerate(parts):
        out[:, h * dim : (h + 1) * dim] = part
    out[:, len(parts) * dim :] = stats


def put_sent(out, parts, stats):
    dim = parts[0].shape[1]
    for h, part in enumerate(parts):
        out[:, h * dim : (h + 1) * dim] = part.astype(out.dtype)
    high = stats.astype(out.dtype)
    at = len(parts) * dim
    out[:, at : at + LANES] = high
    out[:, at + LANES :] = (stats - high.astype(jnp.float32)).astype(out.dtype)


def shift_of(row_max):
    return row_max.astype(jnp.bfloat16).astype(jnp.float32)


def by_head(plan, stacked):
    return [stacked[h * plan.half : (h + 1) * plan.half] for h in range(plan.heads)]


def first_kernel(plan, bias, tile, kv, numer_out, max_out, total_out, scores):
    query = stack_heads(plan, tile)
    top = block_scores(plan, bias, query, kv, 0, plan.half, scores)
    row_max = jnp.max(top, axis=1, keepdims=True)
    total, numer = weigh(plan, scores, 0, row_max, kv[:, plan.dim :])
    numer_out[...] = numer
    max_out[...] = jnp.broadcast_to(row_max, max_out.shape)
    total_out[...] = total


def second_kernel(plan, bias, tile, numer_in, max_in, total_in, kv, send, scores):
    query = stack_heads(plan, tile)
    top = block_scores(plan, bias, query, kv, 1, plan.half, scores)
    row_max = jnp.maximum(jnp.max(top, axis=1, keepdims=True), max_in[...])
    shrink = jnp.exp2((max_in[...] - row_max) * scale_of(plan.dim))
    total, numer = weigh(plan, scores, plan.stored, row_max[:, :1], kv[:, plan.dim :])
    shift = shift_of(row_max)
    grow = jnp.exp2((row_max - shift) * scale_of(plan.dim))
    numer = (numer + numer_in[...] * shrink) * grow
    row_total = jnp.sum((total + total_in[...] * shrink) * grow, axis=1, keepdims=True)
    put_sent(send, by_head(plan, numer), stack_stats(plan, shift, row_total))


def whole_kernel(plan, bias, tile, near, far, keep, scores):
    query = stack_heads(plan, tile)
    top = jnp.maximum(
        block_scores(plan, bias, query, near, 0, 0, scores),
        block_scores(plan, bias, query, far, 1, 0, scores),
    )
    row_max = jnp.max(top, axis=1, keepdims=True)
    total, numer = weigh(plan, scores, 0, row_max, near[:, plan.dim :])
    more_total, more_numer = weigh(plan, scores, plan.stored, row_max, far[:, plan.dim :])
    row_total = jnp.sum(total + more_total, axis=1, keepdims=True)
    put_kept(keep, by_head(plan, numer + more_numer), stack_stats(plan, row_max, row_total))


def combine(heads, dim, left, right):
    feature = heads * dim
    stat_left = left[:, feature:]
    stat_right = right[:, feature : feature + LANES].astype(jnp.float32)
    stat_right = stat_right + right[:, feature + LANES :].astype(jnp.float32)
    top = shift_of(jnp.maximum(stat_left, stat_right))
    is_max = lax.broadcasted_iota(jnp.int32, top.shape, 1) < heads
    shrink_left = jnp.where(is_max, jnp.exp2((stat_left - top) * scale_of(dim)), 0.0)
    shrink_right = jnp.where(is_max, jnp.exp2((stat_right - top) * scale_of(dim)), 0.0)
    moved_left = pltpu.roll(shrink_left, heads, 1)
    moved_right = pltpu.roll(shrink_right, heads, 1)
    stats = jnp.where(is_max, top, stat_left * moved_left + stat_right * moved_right)
    parts = [
        left[:, h * dim : (h + 1) * dim] * shrink_left[:, h : h + 1]
        + right[:, h * dim : (h + 1) * dim].astype(jnp.float32) * shrink_right[:, h : h + 1]
        for h in range(heads)
    ]
    return parts, stats


def merge_kernel(heads, dim, left, right, keep, send):
    parts, stats = combine(heads, dim, left, right)
    half = keep.shape[0]
    put_kept(keep, [part[:half] for part in parts], stats[:half])
    put_sent(send, [part[half:] for part in parts], stats[half:])


def finish_kernel(heads, dim, left, right, out):
    parts, stats = combine(heads, dim, left, right)
    for h, part in enumerate(parts):
        total = stats[:, heads + h : heads + h + 1]
        out[:, h * dim : (h + 1) * dim] = (part / total).astype(out.dtype)


class Plan:
    def __init__(self, **sizes):
        self.__dict__.update(sizes)


def in_vmem(count):
    return [pl.BlockSpec(memory_space=pltpu.VMEM)] * count


def call(kernel, arguments, outputs, scratch=(), megabytes=8):
    return pl.pallas_call(
        kernel,
        out_shape=outputs,
        in_specs=in_vmem(len(arguments)),
        out_specs=tuple(in_vmem(len(outputs))),
        scratch_shapes=scratch,
        compiler_params=pltpu.CompilerParams(vmem_limit_bytes=megabytes * 2**20),
    )(*arguments)


def per_device(queries, key_value, block_lists):
    columns = lax.axis_size("kcol")
    column = lax.axis_index("kcol")
    row_count = lax.axis_size("qrow")
    row_index = lax.axis_index("qrow")
    tok_dev, feature = queries.shape
    dim = key_value.shape[1] // 2
    heads = feature // dim
    stored = key_value.shape[0] // BLK
    groups = block_lists.shape[0]
    masks = [columns >> k for k in range(1, columns.bit_length() - 1)]
    assert columns == 1 << (columns.bit_length() - 1) and row_count == 2

    def across(value, mask):
        pairs = [
            (c * row_count + r, (c ^ mask) * row_count + (r ^ 1))
            for c in range(columns)
            for r in range(row_count)
        ]
        return lax.ppermute(value, AXES, pairs)

    pairs = []
    for c in range(columns):
        pairs += [(c * row_count, (c ^ 1) * row_count + 1), (c * row_count + 1, c * row_count)]
    near = lax.ppermute(key_value, AXES, pairs)
    far = lax.ppermute(near, "qrow", [(0, 1), (1, 0)])

    local = jnp.arange(stored, dtype=jnp.int32)
    ids = jnp.concatenate(
        [(column ^ row_index) * stored + local, (column ^ row_index ^ 1) * stored + local]
    )
    count = 2 * stored
    listed = jnp.any(block_lists[:, :, None] == ids[None, None, :], axis=1)
    bias = jnp.broadcast_to(
        jnp.where(listed, 0.0, hidden_score)[:, :, None], (groups, count, LANES)
    ).astype(jnp.float32)

    staged = lax.optimization_barrier(jnp.pad(queries, ((0, tok_dev), (0, 0))))
    gathered = queries
    for k, mask in enumerate(masks):
        arrived = across(gathered, mask)
        if k == 0 and mask != masks[-1]:
            gathered = staged.at[tok_dev:].set(arrived)
        elif mask != masks[-1]:
            gathered = jnp.concatenate([gathered, arrived], axis=0)
    tokens = 2 * gathered.shape[0]

    plan = Plan(
        half=tokens // 2,
        heads=heads,
        dim=dim,
        groups=groups,
        masks=tuple(masks),
        tok_dev=tok_dev,
        row_count=row_count,
        stored=stored,
        first_query=(stored * columns - groups) * BLK,
    )
    size = tokens // 2
    rows = heads * size
    width = feature + LANES

    def f32(*shape):
        return jax.ShapeDtypeStruct(shape, jnp.float32)

    def sent(count):
        return jax.ShapeDtypeStruct((count, width + LANES), jnp.bfloat16)

    scratch = [pltpu.VMEM((rows, count * BLK), jnp.float32)]
    begun = call(
        functools.partial(first_kernel, plan),
        (bias, arrived, near),
        (f32(rows, dim), f32(rows, LANES), f32(rows, LANES)),
        scratch=scratch,
        megabytes=24,
    )
    (send,) = call(
        functools.partial(second_kernel, plan),
        (bias, arrived, *begun, far),
        (sent(size),),
        scratch=scratch,
        megabytes=24,
    )
    (keep,) = call(
        functools.partial(whole_kernel, plan),
        (bias, gathered, near, far),
        (f32(size, width),),
            scratch=scratch,
        megabytes=24,
    )
    for mask in reversed(masks):
        arrived = across(send, mask)
        if mask != masks[0]:
            size //= 2
            keep, send = call(
                functools.partial(merge_kernel, heads, dim),
                (keep, arrived),
                (f32(size, width), sent(size)),
            )
    (out,) = call(
        functools.partial(finish_kernel, heads, dim),
        (keep, arrived),
        (jax.ShapeDtypeStruct((tok_dev, feature), jnp.bfloat16),),
    )
    return out


def solution(mesh):
    placed = (P(("groups", "kcol", "qrow"), None), P(("groups", "kcol"), None), P("groups", None))
    return jax.shard_map(
        per_device,
        mesh=mesh,
        in_specs=placed,
        out_specs=P(("groups", "kcol", "qrow"), None),
        check_vma=False,
    )
```
